32 devices in a mesh: tm: 4 (over z), det: 8 (over y, x, core).
Axes of the slice: x: 2, y: 2, z: 4, core: 2. Of those that a mesh axis runs over, the one named last changes fastest.
Arguments:
- time_stream: bfloat16 [1024, 32768], P('det', 'tm'), may hold values from -6 to 6
- filter_taps: bfloat16 [1024, 129], P('det'), may hold values from -0.5 to 0.5
- det_precision: bfloat16 [1024, 1024], replicated
- left_weight: float32 [128, 32], replicated, may hold values from -0.046875 to 0.046875
- right_weight: float32 [128, 32], replicated, may hold values from -1 to 1
- frame_tile: int32 [32768, 1], P(('tm', 'det')), may hold values from 0 to 63; in each aligned block of 1024 rows (0 to 1023, 1024 to 2047, ...) at most 24 rows name the same one
- tile_owner: int32 [64], replicated, may hold values from 0 to 31, as said below
- frame_count: int32 [32], P(('tm', 'det')), may hold values from 512 to 1024, as said below
Outputs:
- sky_map: float32 [64, 16384], P(('tm', 'det'))
The draws below stay inside these ranges and needn't reach their ends.
Inputs may be any that keep to these rules, and one draw needn't show every extreme that they name: `frame_tile`: within the frames of one segment (aligned blocks of 1024 rows) no tile is named more than 24 times, a bound that some block reaches. `tile_owner`: every device number is the owner of exactly 2 tiles. `frame_count`: some segment has all 1024 frames live.
All inputs are finite; a program needn't handle non-finite values.
Results may differ from the reference program's by a relative error of at most 0.0041.
Values may be sent and summed in bfloat16 or wider, within the bound.
A program may use at most 64 MiB of HBM per device.

```python
import math
import jax
import jax.numpy as jnp
import numpy as np
from jax import lax

NDET = 1024
HW = 64
FD = 32
FT = 32
TL = 128
SPAN = 1024
TILE_DEV = 2
TAPS = 129
NSAMP = 32768
F_DEV = 1024
NFRAMES = 32768
NTILES = 64
CAP = 24
N_TM = 4
N_DET = 8


def draw_det_precision(key, part):
    first_key, second_key = jax.random.split(jax.random.fold_in(key, 11))
    noise = jax.random.normal(first_key, (NDET, NDET), jnp.float32) * 0.02
    noise = (noise + noise.T) * 0.7071
    diagonal = jax.random.uniform(second_key, (NDET,), jnp.float32, 0.5, 1.5)
    matrix = noise + jnp.diag(diagonal)
    return matrix.astype(jnp.bfloat16)


def draw_tile_owner(key, part):
    order = jax.random.permutation(jax.random.fold_in(key, 23), NTILES)
    return (order // TILE_DEV).astype(jnp.int32)


def draw_frame_count(key, part):
    first_key, second_key = jax.random.split(jax.random.fold_in(key, 37))
    counts = jax.random.randint(first_key, (N_TM * N_DET,), F_DEV // 2, F_DEV + 1, dtype=jnp.int32)
    chosen = jax.random.randint(second_key, (), 0, N_TM * N_DET, dtype=jnp.int32)
    return counts.at[chosen].set(F_DEV).astype(jnp.int32)


def shard_levels(key, dims, cuts, smallest, top_value):
    level = 1.0
    for axis_at, parts in cuts:
        heights = jax.random.uniform(jax.random.fold_in(jax.random.fold_in(key, 6), axis_at), (parts,), jnp.float32, smallest / len(cuts), top_value / len(cuts))
        level = level * jnp.repeat(jnp.exp(heights), dims[axis_at] // parts).reshape((-1,) + (1,) * (len(dims) - 1 - axis_at))
    return level


def routed_block(key, own, number, rows, amount, top, limit, lean):
    ranking = jax.random.permutation(key, amount)
    crowded, usual = load_shares(amount, rows * top, limit, lean, True), load_shares(amount, rows * top, limit, lean, False)
    places = jnp.arange(amount)

    def named(tallies, offset_by):
        used = int((tallies > 0).sum())
        fixed = max(1, used // 4)
        passed = fixed + (places - fixed + offset_by * (used - fixed)) % max(1, amount - fixed)
        return jnp.zeros((amount,), jnp.int32).at[ranking[jnp.where(places < fixed, places, passed)]].set(jnp.asarray(tallies, jnp.int32))

    tallies = jnp.where(number % 4 == 0, named(crowded, number // 4), named(usual, number - number // 4 - 1))
    mixed = jax.random.permutation(jax.random.fold_in(own, 3), amount)
    giver, receiver = mixed[0:amount // 2 * 2:2], mixed[1:amount // 2 * 2:2]
    margin = jnp.minimum(tallies[giver] - 1, limit - tallies[receiver]) // 2
    margin = jnp.where((giver == ranking[0]) | (receiver == ranking[0]) | (tallies[receiver] == 0), 0, jnp.maximum(margin, 0))
    passed = jax.random.randint(jax.random.fold_in(own, 4), (amount // 2,), 0, 1 << 20) % (margin + 1)
    tallies = tallies.at[giver].add(-passed).at[receiver].add(passed)
    members = jnp.searchsorted(jnp.cumsum(tallies), jnp.arange(rows * top), side="right").astype(jnp.int32)
    table = members.reshape(top, rows).T
    table = table[jax.random.permutation(jax.random.fold_in(own, 1), rows)]
    offset_by = jax.random.randint(jax.random.fold_in(own, 2), (rows, 1), 0, top)
    return jnp.take_along_axis(table, (jnp.arange(top)[None, :] + offset_by) % top, axis=1)


def load_shares(number_of, total, limit, lean, full):
    portions = [(1 << 20) // math.isqrt(grade ** lean) + 1 for grade in range(1, number_of + 1)]
    largest = limit if full else min(limit, max(-(-total // number_of), total * portions[0] // sum(portions)))
    least = 1 if total - largest >= number_of - 1 else 0
    holding, rest = [largest] + [least] * (number_of - 1), total - largest - least * (number_of - 1)
    while rest > 0:
        candidates = [i for i in range(1, number_of) if holding[i] < largest] or [i for i in range(1, number_of) if holding[i] < limit]
        mass, remaining = sum([portions[i] for i in candidates]), rest
        for i in candidates:
            addition = min(limit - holding[i], max(1, remaining * portions[i] // mass), rest)
            holding[i] = holding[i] + addition
            rest = rest - addition
    return np.array(holding)


def centred(stream_key, dims, scale, limit, cuts=(), kind=jnp.bfloat16):
    gain = shard_levels(stream_key, dims, cuts, -0.22, 0.18) if cuts else 1.0
    values = jax.random.normal(stream_key, dims, jnp.float32) * scale * gain
    return jnp.minimum(jnp.maximum(values, -limit), limit).astype(kind)


def setup_inputs(seed: int = 0) -> dict:
    key_list = jax.random.split(jax.random.key(seed), 9)
    time_stream = centred(key_list[0], (NDET, NSAMP), 1.0, 6.0, ((0, 8), (1, 4)))
    filter_taps = centred(key_list[1], (NDET, TAPS), TAPS ** -0.5, 0.5, ((0, 8),))
    det_precision = draw_det_precision(jax.random.fold_in(key_list[8], 71), 0)
    left_weight = centred(key_list[3], (TL, FD), (FD * F_DEV // TILE_DEV) ** -0.5, 0.046875, (), jnp.float32)
    right_weight = centred(key_list[4], (TL, FT), FT ** -0.5, 1.0, (), jnp.float32)
    frame_tile_keys = jax.random.split(jax.random.fold_in(key_list[5], 1), NFRAMES // F_DEV)
    frame_tile_turns = jax.random.permutation(jax.random.fold_in(key_list[5], 3), NFRAMES // F_DEV)
    frame_tile = jax.vmap(lambda own, number: routed_block(jax.random.fold_in(key_list[5], 2), own, number, F_DEV, NTILES, 1, CAP, 2))(frame_tile_keys, frame_tile_turns).reshape((NFRAMES, 1))
    tile_owner = draw_tile_owner(jax.random.fold_in(key_list[8], 71), 0)
    frame_count = draw_frame_count(jax.random.fold_in(key_list[8], 71), 0)
    return {"time_stream": time_stream, "filter_taps": filter_taps, "det_precision": det_precision, "left_weight": left_weight, "right_weight": right_weight, "frame_tile": frame_tile, "tile_owner": tile_owner, "frame_count": frame_count}


def toeplitz_block(filter_taps, half_width):
    row_index = jnp.arange(4 * half_width, dtype=jnp.int32)[:, None]
    col_index = jnp.arange(2 * half_width, dtype=jnp.int32)[None, :]
    offset = row_index - col_index
    inside = (offset >= 0) & (offset <= 2 * half_width)
    picked = jnp.take(filter_taps, jnp.clip(offset, 0, 2 * half_width), axis=1)
    return jnp.where(inside[None, :, :], picked, jnp.zeros((), filter_taps.dtype))


def apply_filter(padded, filter_taps, half_width):
    detectors = padded.shape[0]
    blocks = (padded.shape[1] - 2 * half_width) // (2 * half_width)
    pieces = padded.reshape(detectors, blocks + 1, 2 * half_width)
    windows = jnp.concatenate([pieces[:, :-1], pieces[:, 1:]], axis=2)
    matrix = toeplitz_block(filter_taps, half_width)
    result = jnp.einsum("dbj,dji->dbi", windows.astype(jnp.float32), matrix.astype(jnp.float32))
    return result.reshape(detectors, blocks * 2 * half_width)


def frame_rows(whitened):
    groups = whitened.shape[0] // FD
    columns = whitened.shape[1] // FT
    frame_cube = whitened.reshape(groups, FD, columns, FT).transpose(0, 2, 1, 3)
    return frame_cube.reshape(groups * columns, FD * FT)


def owner_rows(tile_owner):
    total_tiles = tile_owner.shape[0]
    same_owner = tile_owner[:, None] == tile_owner[None, :]
    earlier = jnp.arange(total_tiles)[None, :] < jnp.arange(total_tiles)[:, None]
    slot_rank = jnp.sum((same_owner & earlier).astype(jnp.int32), axis=1)
    return (tile_owner * TILE_DEV + slot_rank).astype(jnp.int32)


def project(summed, left_weight, right_weight):
    tiles_here = summed.shape[0]
    frame_cube = summed.reshape(tiles_here, FD, FT)
    partial_value = jnp.einsum("naf,jf->naj", frame_cube, right_weight, precision=lax.Precision.HIGHEST)
    result = jnp.einsum("ia,naj->nij", left_weight, partial_value, precision=lax.Precision.HIGHEST)
    return result.reshape(tiles_here, TL * TL)


def reference(time_stream, filter_taps, det_precision, left_weight, right_weight, frame_tile, tile_owner, frame_count):
    padded = jnp.pad(time_stream, ((0, 0), (HW, HW)))
    tile_index = jnp.arange(NTILES, dtype=jnp.int32)
    frame_index = jnp.arange(F_DEV, dtype=jnp.int32)
    tile_column = frame_tile[:, 0]

    def segment(totals, segment_id):
        offset = (segment_id * SPAN).astype(jnp.int32)
        window = lax.dynamic_slice(padded, (jnp.int32(0), offset), (NDET, SPAN + 2 * HW))
        filtered = apply_filter(window, filter_taps, HW).astype(jnp.bfloat16)
        whitened = jnp.dot(det_precision, filtered, preferred_element_type=jnp.float32).astype(jnp.bfloat16)
        frames = frame_rows(whitened)
        tile_ids = lax.dynamic_slice_in_dim(tile_column, (segment_id * F_DEV).astype(jnp.int32), F_DEV)
        alive_mask = frame_index < frame_count[segment_id]
        onehot = ((tile_ids[:, None] == tile_index[None, :]) & alive_mask[:, None]).astype(jnp.bfloat16)
        added = jnp.einsum("ft,fc->tc", onehot, frames, preferred_element_type=jnp.float32)
        return totals + added, None

    totals, unused = lax.scan(segment, jnp.zeros((NTILES, FD * FT), jnp.float32), jnp.arange(N_TM * N_DET, dtype=jnp.int32))
    ordered = jnp.zeros_like(totals).at[owner_rows(tile_owner)].set(totals)
    return project(ordered, left_weight, right_weight)
```

```python
import functools

import jax
import jax.numpy as jnp
from jax import lax
from jax.experimental import pallas as pl
from jax.experimental.pallas import tpu as pltpu
from jax.sharding import PartitionSpec as P

TILE_DEV = 2
LANES = 128
MESH = pl.DeviceIdType.MESH
VMEM = pltpu.VMEM
F32 = jnp.float32
BF16 = jnp.bfloat16


def owner_rows(tile_owner):
    total_tiles = tile_owner.shape[0]
    same_owner = tile_owner[:, None] == tile_owner[None, :]
    earlier = jnp.arange(total_tiles)[None, :] < jnp.arange(total_tiles)[:, None]
    slot_rank = jnp.sum((same_owner & earlier).astype(jnp.int32), axis=1)
    return tile_owner * TILE_DEV + slot_rank


def edge_kernel(n_tm, n_det, first_ref, last_ref, rows_ref, low_ref, high_ref, all_ref, send_sem, recv_sem, halo_send, halo_recv, own_sem):
    tm, det = lax.axis_index("tm"), lax.axis_index("det")
    has_low, has_high = tm > 0, tm < n_tm - 1
    barrier = pltpu.get_barrier_semaphore()
    for step in range(1, n_det):
        pl.semaphore_signal(barrier, inc=1, device_id=(tm, lax.rem(det + step, n_det)), device_id_type=MESH)

    @pl.when(has_low)
    def _():
        pl.semaphore_signal(barrier, inc=1, device_id=(tm - 1, det), device_id_type=MESH)

    @pl.when(has_high)
    def _():
        pl.semaphore_signal(barrier, inc=1, device_id=(tm + 1, det), device_id_type=MESH)

    pl.semaphore_wait(barrier, n_det - 1 + has_low.astype(jnp.int32) + has_high.astype(jnp.int32))
    down = pltpu.make_async_remote_copy(
        src_ref=first_ref, dst_ref=high_ref, send_sem=halo_send.at[0], recv_sem=halo_recv.at[0],
        device_id=(tm - 1, det), device_id_type=MESH)
    up = pltpu.make_async_remote_copy(
        src_ref=last_ref, dst_ref=low_ref, send_sem=halo_send.at[1], recv_sem=halo_recv.at[1],
        device_id=(tm + 1, det), device_id_type=MESH)

    @pl.when(has_low)
    def _():
        down.start()

    @pl.when(has_high)
    def _():
        up.start()

    copies = []
    for step in range(1, n_det):
        copy = pltpu.make_async_remote_copy(
            src_ref=rows_ref, dst_ref=all_ref.at[det], send_sem=send_sem.at[step], recv_sem=recv_sem.at[step],
            device_id=(tm, lax.rem(det + step, n_det)), device_id_type=MESH)
        copy.start()
        copies.append(copy)
    own = pltpu.make_async_copy(rows_ref, all_ref.at[det], own_sem)
    own.start()

    @pl.when(jnp.logical_not(has_low))
    def _():
        low_ref[...] = jnp.zeros_like(low_ref)

    @pl.when(jnp.logical_not(has_high))
    def _():
        high_ref[...] = jnp.zeros_like(high_ref)

    own.wait()
    for copy in copies:
        copy.wait()

    @pl.when(has_low)
    def _():
        down.wait_send()
        up.wait_recv()

    @pl.when(has_high)
    def _():
        up.wait_send()
        down.wait_recv()


def exchange_edges(n_tm, n_det, first, last, rows):
    vmem = pl.BlockSpec(memory_space=VMEM)
    return pl.pallas_call(
        functools.partial(edge_kernel, n_tm, n_det),
        out_shape=(
            jax.ShapeDtypeStruct(last.shape, last.dtype),
            jax.ShapeDtypeStruct(first.shape, first.dtype),
            jax.ShapeDtypeStruct((n_det,) + rows.shape, rows.dtype),
        ),
        in_specs=[vmem] * 3,
        out_specs=(vmem,) * 3,
        scratch_shapes=[
            pltpu.SemaphoreType.DMA((n_det,)),
            pltpu.SemaphoreType.DMA((n_det,)),
            pltpu.SemaphoreType.DMA((2,)),
            pltpu.SemaphoreType.DMA((2,)),
            pltpu.SemaphoreType.DMA,
        ],
        compiler_params=pltpu.CompilerParams(collective_id=0, has_side_effects=True),
        name="edges",
    )(first, last, rows)


def partial_kernel(
    half, fd, ft, tiles,
    x_ref, low_ref, high_ref, taps_ref, rows_ref, prec_ref, out_ref,
    blocks, result, turned, picks, prec, cells, packed,
):
    dets, samples = x_ref.shape
    width = 2 * half
    nblk = samples // width
    padded = blocks.shape[0] // dets - 1
    groups = prec_ref.shape[0] // fd
    columns = samples // ft
    contract = (((1,), (1,)), ((), ()))

    blocks[0:dets, :] = low_ref[...].astype(F32)
    for b in range(nblk):
        blocks[(b + 1) * dets:(b + 2) * dets, :] = x_ref[:, b * width:(b + 1) * width].astype(F32)
    blocks[(nblk + 1) * dets:(nblk + 2) * dets, :] = high_ref[...].astype(F32)
    blocks[(nblk + 2) * dets:, :] = jnp.zeros((blocks.shape[0] - (nblk + 2) * dets, width), F32)

    rows = jnp.concatenate([rows_ref[s] for s in range(rows_ref.shape[0])], axis=1)
    tile = lax.broadcasted_iota(jnp.int32, (tiles, columns), 0)
    for g in range(groups):
        picks[g * tiles:(g + 1) * tiles, :] = jnp.where(tile == rows[g:g + 1, :], 1.0, 0.0).astype(BF16)
        prec[:, g * dets:(g + 1) * dets] = prec_ref[g * fd:(g + 1) * fd, :]

    unroll = 4

    def filter_step(step, carry):
        for k in range(unroll):
            d = step * unroll + k
            spread = jnp.broadcast_to(taps_ref[pl.ds(d, 1), :], (width, 2 * width))
            matrix = pltpu.roll(spread, 0, 1, stride=1, stride_axis=0).astype(BF16)
            lower = blocks[pl.ds(d, padded, stride=dets), :]
            upper = blocks[pl.ds(d + dets, padded, stride=dets), :]
            window = jnp.concatenate([lower, upper], axis=1).astype(BF16)
            result[pl.ds(d, padded, stride=dets), :] = lax.dot_general(
                window, matrix, contract, preferred_element_type=F32)
        return carry

    lax.fori_loop(0, dets // unroll, filter_step, 0)

    def turn_step(b, carry):
        at = pl.multiple_of(b * dets, dets)
        to = pl.multiple_of(b * width, width)
        turned[pl.ds(to, width), :] = result[pl.ds(at, dets), :].T
        return carry

    lax.fori_loop(0, nblk + 1, turn_step, 0)

    share = 4

    def sum_step(pair, carry):
        f = pair * 2
        left = turned[pl.ds(half + f, columns, stride=ft), :]
        right = turned[pl.ds(half + f + 1, columns, stride=ft), :]
        weight = jnp.concatenate([left, right], axis=1).astype(BF16)
        at = pl.multiple_of(f * tiles, tiles)
        for g in range(0, groups, share):
            sums = jnp.dot(picks[g * tiles:(g + share) * tiles, :], weight, preferred_element_type=F32).astype(BF16)
            for k in range(share):
                for side in range(2):
                    cells[pl.ds(at + side * tiles, tiles), (g + k) * dets:(g + k + 1) * dets] = (
                        sums[k * tiles:(k + 1) * tiles, side * dets:(side + 1) * dets])
        return carry

    lax.fori_loop(0, ft // 2, sum_step, 0)

    across = LANES // fd
    low = ft // across

    def product_step(u, carry):
        parts = []
        for v in range(across):
            at = pl.multiple_of((v * low + u) * tiles, tiles)
            parts.append(lax.dot_general(cells[pl.ds(at, tiles), :], prec[...], contract, preferred_element_type=F32))
        packed[pl.ds(pl.multiple_of(u * tiles, tiles), tiles), :] = jnp.concatenate(parts, axis=1)
        return carry

    lax.fori_loop(0, low, product_step, 0)
    for owner in range(out_ref.shape[0]):
        mine = [packed[pl.ds(owner * TILE_DEV + k, low, stride=tiles), :] for k in range(TILE_DEV)]
        out_ref[owner] = jnp.concatenate(mine, axis=0).astype(out_ref.dtype)


def partial_sums(x, low, high, taps, rows, precision, half, fd, ft, tiles):
    dets, samples = x.shape
    width = 2 * half
    padded = -(-(samples // width + 1) // 8) * 8
    groups = precision.shape[0] // fd
    widened = jnp.pad(taps.astype(F32), ((0, 0), (0, 2 * width - taps.shape[1])))
    vmem = pl.BlockSpec(memory_space=VMEM)
    across = LANES // fd
    return pl.pallas_call(
        functools.partial(partial_kernel, half, fd, ft, tiles),
        out_shape=jax.ShapeDtypeStruct((tiles // TILE_DEV, TILE_DEV * ft // across, LANES), BF16),
        in_specs=[vmem] * 6,
        out_specs=vmem,
        scratch_shapes=[
            VMEM(((padded + 1) * dets, width), F32),
            VMEM((padded * dets, width), F32),
            VMEM((samples + width, dets), F32),
            VMEM((groups * tiles, samples // ft), BF16),
            VMEM((fd, groups * dets), BF16),
            VMEM((ft * tiles, groups * dets), BF16),
            VMEM((ft // across * tiles, LANES), F32),
        ],
        compiler_params=pltpu.CompilerParams(vmem_limit_bytes=60 * 1024 * 1024),
        name="partials",
    )(x, low, high, widened, rows, precision)


def plain_partial_sums(x, low, high, taps, rows, precision, half, fd, ft, tiles):
    dets, samples = x.shape
    width = 2 * half
    groups = precision.shape[0] // fd
    blocks = samples // width
    padded = jnp.concatenate([low[:, -half:], x, high[:, :half]], axis=1).reshape(dets, blocks + 1, width)
    length = 4 * half + 1
    tiled = jnp.broadcast_to(jnp.pad(taps, ((0, 0), (0, length - taps.shape[1])))[:, None, :], (dets, width, length))
    matrix = tiled.reshape(dets, width * length)[:, :width * 2 * width].reshape(dets, width, 2 * width)
    near = jnp.einsum("dbj,dij->dbi", padded, matrix[:, :, :width], preferred_element_type=F32)
    far = jnp.einsum("dbj,dij->dbi", padded, matrix[:, :, width:], preferred_element_type=F32)
    filtered = (near[:, :-1] + far[:, 1:]).astype(BF16).reshape(dets, samples // ft, ft)
    picks = (rows.transpose(1, 0, 2).reshape(groups, 1, -1) == jnp.arange(tiles, dtype=jnp.int32)[None, :, None]).astype(BF16)
    sums = jnp.einsum("gkt,dtf->gkfd", picks, filtered, preferred_element_type=F32).astype(BF16)
    out = jnp.einsum("gkfd,gad->kfa", sums, precision.reshape(groups, fd, dets), preferred_element_type=F32)
    across = LANES // fd
    low_part = ft // across
    out = out.reshape(tiles, across, low_part, fd).transpose(0, 2, 1, 3)
    return out.reshape(tiles // TILE_DEV, TILE_DEV * low_part, LANES).astype(BF16)


def gather_kernel(n_tm, n_det, part_ref, left_ref, right_ref, out_ref, held, send_sem, recv_sem, own_sem):
    tm, det = lax.axis_index("tm"), lax.axis_index("det")
    count = n_tm * n_det
    me = tm * n_det + det
    fd = left_ref.shape[0]
    barrier = pltpu.get_barrier_semaphore()

    def peer(step):
        other = lax.rem(me + step, count)
        return other, (other // n_det, lax.rem(other, n_det))

    for step in range(1, count):
        pl.semaphore_signal(barrier, inc=1, device_id=peer(step)[1], device_id_type=MESH)
    own = pltpu.make_async_copy(part_ref.at[me], held.at[me], own_sem)
    own.start()
    pl.semaphore_wait(barrier, count - 1)
    copies = []
    for step in range(1, count):
        other, where = peer(step)
        copy = pltpu.make_async_remote_copy(
            src_ref=part_ref.at[other], dst_ref=held.at[me], send_sem=send_sem.at[step], recv_sem=recv_sem.at[step],
            device_id=where, device_id_type=MESH)
        copy.start()
        copies.append(copy)
    own.wait()
    for copy in copies:
        copy.wait()
    total = jnp.sum(held[...].astype(F32), axis=0)
    low = total.shape[0] // TILE_DEV
    across = total.shape[1] // fd
    for k in range(TILE_DEV):
        tile = total[k * low:(k + 1) * low, :]
        stacked = jnp.concatenate([tile[:, v * fd:(v + 1) * fd] for v in range(across)], axis=0)
        rows = jnp.dot(stacked, left_ref[...], precision=lax.Precision.HIGHEST, preferred_element_type=F32)
        out_ref[k] = lax.dot_general(
            rows, right_ref[...], (((0,), (0,)), ((), ())), precision=lax.Precision.HIGHEST,
            preferred_element_type=F32)


def gather_tiles(n_tm, n_det, part, left, right):
    count = n_tm * n_det
    vmem = pl.BlockSpec(memory_space=VMEM)
    return pl.pallas_call(
        functools.partial(gather_kernel, n_tm, n_det),
        out_shape=jax.ShapeDtypeStruct((TILE_DEV, left.shape[1], right.shape[1]), F32),
        in_specs=[vmem] * 3,
        out_specs=vmem,
        scratch_shapes=[
            VMEM(part.shape, part.dtype),
            pltpu.SemaphoreType.DMA((count,)),
            pltpu.SemaphoreType.DMA((count,)),
            pltpu.SemaphoreType.DMA,
        ],
        compiler_params=pltpu.CompilerParams(collective_id=1, has_side_effects=True),
        name="gather",
    )(part, left, right)


def local(
    n_tm, n_det,
    time_stream, filter_taps, det_precision, left_weight, right_weight, frame_tile, tile_owner, frame_count,
):
    half = filter_taps.shape[1] // 2
    width = 2 * half
    fd, ft = left_weight.shape[1], right_weight.shape[1]
    dets = time_stream.shape[0]
    tiles = tile_owner.shape[0]
    frames = frame_tile.shape[0]
    groups = det_precision.shape[0] // fd
    on_tile = frame_tile == jnp.arange(tiles, dtype=jnp.int32)[None, :]
    dest_row = jnp.sum(jnp.where(on_tile, owner_rows(tile_owner)[None, :], 0), axis=1)
    alive = jnp.arange(frames, dtype=jnp.int32) < frame_count[0]
    rows = jnp.where(alive, dest_row, -1).reshape(groups, frames // groups)
    low, high, rows = exchange_edges(n_tm, n_det, time_stream[:, :width], time_stream[:, -width:], rows)
    precision = lax.dynamic_slice_in_dim(det_precision, lax.axis_index("det") * dets, dets, axis=1)
    form = partial_sums if dets % LANES == 0 else plain_partial_sums
    part = form(time_stream, low, high, filter_taps, rows, precision, half, fd, ft, tiles)
    sky = gather_tiles(n_tm, n_det, part, left_weight.T, right_weight.T)
    return sky.reshape(TILE_DEV, -1)


def solution(mesh):
    return jax.shard_map(
        functools.partial(local, mesh.shape["tm"], mesh.shape["det"]),
        mesh=mesh,
        in_specs=(
            P("det", "tm"),
            P("det", None),
            P(),
            P(),
            P(),
            P(("tm", "det"), None),
            P(),
            P(("tm", "det")),
        ),
        out_specs=P(("tm", "det"), None),
        check_vma=False,
    )
```

```python
import functools

import jax
import jax.numpy as jnp
from jax import lax
from jax.experimental import pallas as pl
from jax.experimental.pallas import tpu as pltpu
from jax.sharding import PartitionSpec as P

TILE_DEV = 2
LANES = 128
MESH = pl.DeviceIdType.MESH
VMEM = pltpu.VMEM
F32 = jnp.float32
BF16 = jnp.bfloat16


def owner_rows(tile_owner):
    total_tiles = tile_owner.shape[0]
    same_owner = tile_owner[:, None] == tile_owner[None, :]
    earlier = jnp.arange(total_tiles)[None, :] < jnp.arange(total_tiles)[:, None]
    slot_rank = jnp.sum((same_owner & earlier).astype(jnp.int32), axis=1)
    return tile_owner * TILE_DEV + slot_rank


def edge_kernel(n_tm, n_det, width, x_ref, tile_ref, count_ref, low_ref, high_ref, all_ref, rows_ref, send_sem, recv_sem, halo_send, halo_recv, own_sem):
    tm, det = lax.axis_index("tm"), lax.axis_index("det")
    has_low, has_high = tm > 0, tm < n_tm - 1
    barrier = pltpu.get_barrier_semaphore()
    for step in range(1, n_det):
        pl.semaphore_signal(barrier, inc=1, device_id=(tm, lax.rem(det + step, n_det)), device_id_type=MESH)

    @pl.when(has_low)
    def _():
        pl.semaphore_signal(barrier, inc=1, device_id=(tm - 1, det), device_id_type=MESH)

    @pl.when(has_high)
    def _():
        pl.semaphore_signal(barrier, inc=1, device_id=(tm + 1, det), device_id_type=MESH)

    tile = tile_ref[...]
    frame = lax.broadcasted_iota(jnp.int32, tile.shape, 0) * tile.shape[1] + lax.broadcasted_iota(jnp.int32, tile.shape, 1)
    rows_ref[...] = jnp.where(frame < count_ref[0], tile, -1)
    pl.semaphore_wait(barrier, n_det - 1 + has_low.astype(jnp.int32) + has_high.astype(jnp.int32))
    down = pltpu.make_async_remote_copy(
        src_ref=x_ref.at[:, 0:width], dst_ref=high_ref, send_sem=halo_send.at[0], recv_sem=halo_recv.at[0],
        device_id=(tm - 1, det), device_id_type=MESH)
    up = pltpu.make_async_remote_copy(
        src_ref=x_ref.at[:, x_ref.shape[1] - width:], dst_ref=low_ref, send_sem=halo_send.at[1], recv_sem=halo_recv.at[1],
        device_id=(tm + 1, det), device_id_type=MESH)

    @pl.when(has_low)
    def _():
        down.start()

    @pl.when(has_high)
    def _():
        up.start()

    copies = []
    for step in range(1, n_det):
        copy = pltpu.make_async_remote_copy(
            src_ref=rows_ref, dst_ref=all_ref.at[det], send_sem=send_sem.at[step], recv_sem=recv_sem.at[step],
            device_id=(tm, lax.rem(det + step, n_det)), device_id_type=MESH)
        copy.start()
        copies.append(copy)
    own = pltpu.make_async_copy(rows_ref, all_ref.at[det], own_sem)
    own.start()

    @pl.when(jnp.logical_not(has_low))
    def _():
        low_ref[...] = jnp.zeros_like(low_ref)

    @pl.when(jnp.logical_not(has_high))
    def _():
        high_ref[...] = jnp.zeros_like(high_ref)

    own.wait()
    for copy in copies:
        copy.wait()

    @pl.when(has_low)
    def _():
        down.wait_send()
        up.wait_recv()

    @pl.when(has_high)
    def _():
        up.wait_send()
        down.wait_recv()


def exchange_edges(n_tm, n_det, width, x, tile, count):
    vmem = pl.BlockSpec(memory_space=VMEM)
    halo = jax.ShapeDtypeStruct((x.shape[0], width), x.dtype)
    return pl.pallas_call(
        functools.partial(edge_kernel, n_tm, n_det, width),
        out_shape=(halo, halo, jax.ShapeDtypeStruct((n_det,) + tile.shape, tile.dtype)),
        in_specs=[pl.BlockSpec(memory_space=pl.ANY), vmem, pl.BlockSpec(memory_space=pltpu.SMEM)],
        out_specs=(vmem,) * 3,
        scratch_shapes=[
            VMEM(tile.shape, tile.dtype),
            pltpu.SemaphoreType.DMA((n_det,)),
            pltpu.SemaphoreType.DMA((n_det,)),
            pltpu.SemaphoreType.DMA((2,)),
            pltpu.SemaphoreType.DMA((2,)),
            pltpu.SemaphoreType.DMA,
        ],
        compiler_params=pltpu.CompilerParams(collective_id=0, has_side_effects=True),
        name="edges",
    )(x, tile, count)


def divisor(number, most):
    return max(d for d in range(1, most + 1) if number % d == 0)


def partial_body(
    half, fd, ft, tiles,
    x_ref, low_ref, high_ref, tapst_ref, rows_ref, owner_ref, prec_ref, out_ref,
    wide, taps_ref, blocks, result, turned, picks, prec, cells, packed,
):
    dets, samples = x_ref.shape
    width = 2 * half
    nblk = samples // width
    padded = blocks.shape[0] // dets - 1
    groups = prec_ref.shape[0] // fd
    columns = samples // ft
    contract = (((1,), (1,)), ((), ()))

    blocks[0:dets, :] = low_ref[...].astype(F32)
    for b in range(nblk):
        blocks[(b + 1) * dets:(b + 2) * dets, :] = x_ref[:, b * width:(b + 1) * width].astype(F32)
    blocks[(nblk + 1) * dets:(nblk + 2) * dets, :] = high_ref[...].astype(F32)
    blocks[(nblk + 2) * dets:, :] = jnp.zeros((blocks.shape[0] - (nblk + 2) * dets, width), F32)

    wide[...] = jnp.zeros(wide.shape, F32)
    wide[0:tapst_ref.shape[0], :] = tapst_ref[...].astype(F32)
    taps_ref[...] = wide[...].T

    across_owner = jnp.broadcast_to(owner_ref[...].astype(F32), (tiles, tiles))
    down = lax.broadcasted_iota(jnp.int32, (tiles, tiles), 0)
    across_tile = lax.broadcasted_iota(jnp.int32, (tiles, tiles), 1)
    earlier = (across_owner.T == across_owner) & (down < across_tile)
    rank = jnp.sum(jnp.where(earlier, 1.0, 0.0), axis=0, keepdims=True)
    place = across_owner * TILE_DEV + rank
    order = jnp.sum(jnp.where(place == down.astype(F32), across_tile.astype(F32), 0.0), axis=1, keepdims=True)
    order = jnp.broadcast_to(order, (tiles, columns))
    per_row = rows_ref.shape[2] // (columns // rows_ref.shape[0])
    span = rows_ref.shape[2] // per_row
    for q in range(per_row):
        rows = jnp.concatenate([rows_ref[s][:, q * span:(q + 1) * span] for s in range(rows_ref.shape[0])], axis=1).astype(F32)
        for r in range(rows.shape[0]):
            g = r * per_row + q
            picks[g * tiles:(g + 1) * tiles, :] = jnp.where(order == rows[r:r + 1, :], 1.0, 0.0).astype(BF16)
    for g in range(groups):
        prec[:, g * dets:(g + 1) * dets] = prec_ref[g * fd:(g + 1) * fd, :]

    unroll = divisor(dets, 16)

    def filter_step(step, carry):
        for k in range(unroll):
            d = step * unroll + k
            spread = jnp.broadcast_to(taps_ref[pl.ds(d, 1), :], (width, 2 * width))
            matrix = pltpu.roll(spread, 0, 1, stride=1, stride_axis=0).astype(BF16)
            lower = blocks[pl.ds(d, padded, stride=dets), :]
            upper = blocks[pl.ds(d + dets, padded, stride=dets), :]
            window = jnp.concatenate([lower, upper], axis=1).astype(BF16)
            result[pl.ds(d, padded, stride=dets), :] = lax.dot_general(
                window, matrix, contract, preferred_element_type=F32)
        return carry

    lax.fori_loop(0, dets // unroll, filter_step, 0)

    turns = divisor(nblk + 1, 16)

    def turn_step(step, carry):
        for k in range(turns):
            b = step * turns + k
            at = pl.multiple_of(b * dets, dets)
            to = pl.multiple_of(b * width, width)
            turned[pl.ds(to, width), :] = result[pl.ds(at, dets), :].astype(BF16).T.astype(F32)
        return carry

    lax.fori_loop(0, (nblk + 1) // turns, turn_step, 0)

    share = 4

    pairs = divisor(ft // 2, 4)

    def sum_pair(pair):
        f = pair * 2
        left = turned[pl.ds(half + f, columns, stride=ft), :]
        right = turned[pl.ds(half + f + 1, columns, stride=ft), :]
        weight = jnp.concatenate([left, right], axis=1).astype(BF16)
        at = pl.multiple_of(f * tiles, tiles)
        for g in range(0, groups, share):
            sums = jnp.dot(picks[g * tiles:(g + share) * tiles, :], weight, preferred_element_type=F32).astype(BF16)
            for k in range(share):
                for side in range(2):
                    cells[pl.ds(at + side * tiles, tiles), (g + k) * dets:(g + k + 1) * dets] = (
                        sums[k * tiles:(k + 1) * tiles, side * dets:(side + 1) * dets])

    def sum_step(step, carry):
        for k in range(pairs):
            sum_pair(step * pairs + k)
        return carry

    lax.fori_loop(0, ft // 2 // pairs, sum_step, 0)

    across = LANES // fd
    low = ft // across

    def product_step(u, carry):
        parts = []
        for v in range(across):
            at = pl.multiple_of((v * low + u) * tiles, tiles)
            parts.append(lax.dot_general(cells[pl.ds(at, tiles), :], prec[...], contract, preferred_element_type=F32))
        packed[pl.ds(pl.multiple_of(u * tiles, tiles), tiles), :] = jnp.concatenate(parts, axis=1)
        return carry

    lax.fori_loop(0, low, product_step, 0, unroll=2)
    for owner in range(out_ref.shape[0]):
        mine = [packed[pl.ds(owner * TILE_DEV + k, low, stride=tiles), :] for k in range(TILE_DEV)]
        out_ref[owner] = jnp.concatenate(mine, axis=0).astype(out_ref.dtype)


def partial_scratch(half, fd, ft, tiles, x, precision):
    dets, samples = x.shape
    width = 2 * half
    padded = -(-(samples // width + 1) // 8) * 8
    groups = precision.shape[0] // fd
    across = LANES // fd
    return [
        VMEM((2 * width, dets), F32),
        VMEM((dets, 2 * width), F32),
        VMEM(((padded + 1) * dets, width), F32),
        VMEM((padded * dets, width), F32),
        VMEM((samples + width, dets), F32),
        VMEM((groups * tiles, samples // ft), BF16),
        VMEM((fd, groups * dets), BF16),
        VMEM((ft * tiles, groups * dets), BF16),
        VMEM((ft // across * tiles, LANES), F32),
    ]


def part_shape(fd, ft, tiles):
    return (tiles // TILE_DEV, TILE_DEV * ft // (LANES // fd), LANES)


def plain_partial_sums(x, low, high, taps, rows, owner, precision, half, fd, ft, tiles):
    dets, samples = x.shape
    width = 2 * half
    groups = precision.shape[0] // fd
    blocks = samples // width
    padded = jnp.concatenate([low[:, -half:], x, high[:, :half]], axis=1).reshape(dets, blocks + 1, width)
    length = 4 * half + 1
    tiled = jnp.broadcast_to(jnp.pad(taps, ((0, 0), (0, length - taps.shape[1])))[:, None, :], (dets, width, length))
    matrix = tiled.reshape(dets, width * length)[:, :width * 2 * width].reshape(dets, width, 2 * width)
    near = jnp.einsum("dbj,dij->dbi", padded, matrix[:, :, :width], preferred_element_type=F32)
    far = jnp.einsum("dbj,dij->dbi", padded, matrix[:, :, width:], preferred_element_type=F32)
    filtered = (near[:, :-1] + far[:, 1:]).astype(BF16).reshape(dets, samples // ft, ft)
    order = jnp.argsort(owner_rows(owner)).astype(jnp.int32)
    rows = rows.reshape(rows.shape[0], groups, -1).transpose(1, 0, 2).reshape(groups, 1, -1)
    picks = (rows == order[None, :, None]).astype(BF16)
    sums = jnp.einsum("gkt,dtf->gkfd", picks, filtered, preferred_element_type=F32).astype(BF16)
    out = jnp.einsum("gkfd,gad->kfa", sums, precision.reshape(groups, fd, dets), preferred_element_type=F32)
    across = LANES // fd
    low_part = ft // across
    out = out.reshape(tiles, across, low_part, fd).transpose(0, 2, 1, 3)
    return out.reshape(tiles // TILE_DEV, TILE_DEV * low_part, LANES).astype(BF16)


def peer(me, step, n_tm, n_det):
    other = lax.rem(me + step, n_tm * n_det)
    return other, (other // n_det, lax.rem(other, n_det))


def greet(n_tm, n_det):
    me = lax.axis_index("tm") * n_det + lax.axis_index("det")
    barrier = pltpu.get_barrier_semaphore()
    for step in range(1, n_tm * n_det):
        pl.semaphore_signal(barrier, inc=1, device_id=peer(me, step, n_tm, n_det)[1], device_id_type=MESH)
    return me, barrier


def gather_body(n_tm, n_det, me, barrier, part_ref, left_ref, right_ref, out_ref, held, send_sem, recv_sem, own_sem):
    count = n_tm * n_det
    fd = left_ref.shape[0]
    pl.semaphore_wait(barrier, count - 1)
    copies = []
    for step in range(1, count):
        other, where = peer(me, step, n_tm, n_det)
        copy = pltpu.make_async_remote_copy(
            src_ref=part_ref.at[other], dst_ref=held.at[me], send_sem=send_sem.at[step], recv_sem=recv_sem.at[step],
            device_id=where, device_id_type=MESH)
        copy.start()
        copies.append(copy)
    own = pltpu.make_async_copy(part_ref.at[me], held.at[me], own_sem)
    own.start()
    own.wait()
    for copy in copies:
        copy.wait()
    total = jnp.sum(held[...].astype(F32), axis=0)
    low = total.shape[0] // TILE_DEV
    across = total.shape[1] // fd
    for k in range(TILE_DEV):
        tile = total[k * low:(k + 1) * low, :]
        stacked = jnp.concatenate([tile[:, v * fd:(v + 1) * fd] for v in range(across)], axis=0)
        rows = jnp.dot(stacked, left_ref[...], precision=lax.Precision.HIGHEST, preferred_element_type=F32)
        out_ref[k] = lax.dot_general(
            rows, right_ref[...], (((0,), (0,)), ((), ())), precision=lax.Precision.HIGHEST,
            preferred_element_type=F32)


def gather_kernel(n_tm, n_det, part_ref, left_ref, right_ref, out_ref, *scratch):
    me, barrier = greet(n_tm, n_det)
    gather_body(n_tm, n_det, me, barrier, part_ref, left_ref, right_ref, out_ref, *scratch)


def whole_kernel(n_tm, n_det, sizes, *refs):
    ins, (left_ref, right_ref, out_ref, part), rest = refs[:7], refs[7:11], refs[11:]
    me, barrier = greet(n_tm, n_det)
    partial_body(*sizes, *ins, part, *rest[:-4])
    gather_body(n_tm, n_det, me, barrier, part, left_ref, right_ref, out_ref, *rest[-4:])


def gather_scratch(count, shape):
    return [
        VMEM(shape, BF16),
        pltpu.SemaphoreType.DMA((count,)),
        pltpu.SemaphoreType.DMA((count,)),
        pltpu.SemaphoreType.DMA,
    ]


def call(kernel, inputs, scratch, tall, name):
    vmem = pl.BlockSpec(memory_space=VMEM)
    return pl.pallas_call(
        kernel,
        out_shape=jax.ShapeDtypeStruct((TILE_DEV,) + tall, F32),
        in_specs=[vmem] * len(inputs),
        out_specs=vmem,
        scratch_shapes=scratch,
        compiler_params=pltpu.CompilerParams(
            collective_id=1, has_side_effects=True, vmem_limit_bytes=60 * 1024 * 1024),
        name=name,
    )(*inputs)


def local(
    n_tm, n_det,
    time_stream, filter_taps, det_precision, left_weight, right_weight, frame_tile, tile_owner, frame_count,
):
    half = filter_taps.shape[1] // 2
    fd, ft = left_weight.shape[1], right_weight.shape[1]
    dets = time_stream.shape[0]
    tiles = tile_owner.shape[0]
    count = n_tm * n_det
    low, high, rows = exchange_edges(n_tm, n_det, 2 * half, time_stream, frame_tile.reshape(-1, LANES), frame_count)
    precision = lax.dynamic_slice_in_dim(det_precision, lax.axis_index("det") * dets, dets, axis=1)
    sizes = (half, fd, ft, tiles)
    shape = part_shape(fd, ft, tiles)
    tall = (left_weight.shape[0], right_weight.shape[0])
    weights = (left_weight.T, right_weight.T)
    if dets % LANES == 0:
        inputs = (time_stream, low, high, filter_taps.T, rows, tile_owner.reshape(1, -1), precision) + weights
        scratch = [VMEM(shape, BF16)] + partial_scratch(half, fd, ft, tiles, time_stream, precision)
        sky = call(functools.partial(whole_kernel, n_tm, n_det, sizes), inputs, scratch + gather_scratch(count, shape), tall, "whole")
    else:
        part = plain_partial_sums(time_stream, low, high, filter_taps, rows, tile_owner, precision, *sizes)
        sky = call(functools.partial(gather_kernel, n_tm, n_det), (part,) + weights, gather_scratch(count, shape), tall, "gather")
    return sky.reshape(TILE_DEV, -1)


def solution(mesh):
    return jax.shard_map(
        functools.partial(local, mesh.shape["tm"], mesh.shape["det"]),
        mesh=mesh,
        in_specs=(
            P("det", "tm"),
            P("det", None),
            P(),
            P(),
            P(),
            P(("tm", "det"), None),
            P(),
            P(("tm", "det")),
        ),
        out_specs=P(("tm", "det"), None),
        check_vma=False,
    )
```

```python
import functools

import jax
import jax.numpy as jnp
from jax import lax
from jax.experimental import pallas as pl
from jax.experimental.pallas import tpu as pltpu
from jax.sharding import PartitionSpec as P

TILE_DEV = 2
LANES = 128
MESH = pl.DeviceIdType.MESH
VMEM = pltpu.VMEM
F32 = jnp.float32
BF16 = jnp.bfloat16


def owner_rows(tile_owner):
    total_tiles = tile_owner.shape[0]
    same_owner = tile_owner[:, None] == tile_owner[None, :]
    earlier = jnp.arange(total_tiles)[None, :] < jnp.arange(total_tiles)[:, None]
    slot_rank = jnp.sum((same_owner & earlier).astype(jnp.int32), axis=1)
    return tile_owner * TILE_DEV + slot_rank


def start_edges(n_tm, n_det, width, x_ref, low_ref, high_ref, all_ref, rows_ref, send_sem, recv_sem, halo_send, halo_recv, own_sem):
    tm, det = lax.axis_index("tm"), lax.axis_index("det")
    has_low, has_high = tm > 0, tm < n_tm - 1
    down = pltpu.make_async_remote_copy(
        src_ref=x_ref.at[:, 0:width], dst_ref=high_ref, send_sem=halo_send.at[0], recv_sem=halo_recv.at[0],
        device_id=(tm - 1, det), device_id_type=MESH)
    up = pltpu.make_async_remote_copy(
        src_ref=x_ref.at[:, x_ref.shape[1] - width:], dst_ref=low_ref, send_sem=halo_send.at[1], recv_sem=halo_recv.at[1],
        device_id=(tm + 1, det), device_id_type=MESH)

    @pl.when(has_low)
    def _():
        down.start()

    @pl.when(has_high)
    def _():
        up.start()

    copies = []
    for step in range(1, n_det):
        copy = pltpu.make_async_remote_copy(
            src_ref=rows_ref, dst_ref=all_ref.at[det], send_sem=send_sem.at[step], recv_sem=recv_sem.at[step],
            device_id=(tm, lax.rem(det + step, n_det)), device_id_type=MESH)
        copy.start()
        copies.append(copy)
    own = pltpu.make_async_copy(rows_ref, all_ref.at[det], own_sem)
    own.start()

    @pl.when(jnp.logical_not(has_low))
    def _():
        low_ref[...] = jnp.zeros_like(low_ref)

    @pl.when(jnp.logical_not(has_high))
    def _():
        high_ref[...] = jnp.zeros_like(high_ref)

    def finish():
        own.wait()
        for copy in copies:
            copy.wait()

        @pl.when(has_low)
        def _():
            down.wait_send()
            up.wait_recv()

        @pl.when(has_high)
        def _():
            up.wait_send()
            down.wait_recv()

    return finish


def live_rows(tile_ref, count_ref, rows_ref):
    tile = tile_ref[...]
    frame = lax.broadcasted_iota(jnp.int32, tile.shape, 0) * tile.shape[1] + lax.broadcasted_iota(jnp.int32, tile.shape, 1)
    rows_ref[...] = jnp.where(frame < count_ref[0], tile, -1)


def edge_kernel(n_tm, n_det, width, x_ref, tile_ref, count_ref, low_ref, high_ref, all_ref, rows_ref, *sems):
    tm, det = lax.axis_index("tm"), lax.axis_index("det")
    has_low, has_high = tm > 0, tm < n_tm - 1
    barrier = pltpu.get_barrier_semaphore()
    for step in range(1, n_det):
        pl.semaphore_signal(barrier, inc=1, device_id=(tm, lax.rem(det + step, n_det)), device_id_type=MESH)

    @pl.when(has_low)
    def _():
        pl.semaphore_signal(barrier, inc=1, device_id=(tm - 1, det), device_id_type=MESH)

    @pl.when(has_high)
    def _():
        pl.semaphore_signal(barrier, inc=1, device_id=(tm + 1, det), device_id_type=MESH)

    live_rows(tile_ref, count_ref, rows_ref)
    pl.semaphore_wait(barrier, n_det - 1 + has_low.astype(jnp.int32) + has_high.astype(jnp.int32))
    start_edges(n_tm, n_det, width, x_ref, low_ref, high_ref, all_ref, rows_ref, *sems)()


def edge_sems(n_det):
    return [
        pltpu.SemaphoreType.DMA((n_det,)),
        pltpu.SemaphoreType.DMA((n_det,)),
        pltpu.SemaphoreType.DMA((2,)),
        pltpu.SemaphoreType.DMA((2,)),
        pltpu.SemaphoreType.DMA,
    ]


def exchange_edges(n_tm, n_det, width, x, tile, count):
    vmem = pl.BlockSpec(memory_space=VMEM)
    halo = jax.ShapeDtypeStruct((x.shape[0], width), x.dtype)
    return pl.pallas_call(
        functools.partial(edge_kernel, n_tm, n_det, width),
        out_shape=(halo, halo, jax.ShapeDtypeStruct((n_det,) + tile.shape, tile.dtype)),
        in_specs=[pl.BlockSpec(memory_space=pl.ANY), vmem, pl.BlockSpec(memory_space=pltpu.SMEM)],
        out_specs=(vmem,) * 3,
        scratch_shapes=[
            VMEM(tile.shape, tile.dtype),
        ] + edge_sems(n_det),
        compiler_params=pltpu.CompilerParams(collective_id=0, has_side_effects=True),
        name="edges",
    )(x, tile, count)


def divisor(number, most):
    return max(d for d in range(1, most + 1) if number % d == 0)


def partial_body(
    half, fd, ft, tiles, exchange,
    x_hbm, tapst_ref, owner_ref, prec_hbm, low_ref, high_ref, rows_ref, out_ref,
    x_ref, prec_ref, load_sem, wide, taps_ref, blocks, result, turned, picks, prec, cells, packed,
):
    dets, samples = x_ref.shape
    first = pl.multiple_of(lax.axis_index("det") * dets, dets)
    loads = [
        pltpu.make_async_copy(x_hbm, x_ref, load_sem.at[0]),
        pltpu.make_async_copy(prec_hbm.at[:, pl.ds(first, dets)], prec_ref, load_sem.at[1]),
    ]
    for load in loads:
        load.start()
    width = 2 * half
    nblk = samples // width
    padded = blocks.shape[0] // dets - 1
    groups = prec_ref.shape[0] // fd
    columns = samples // ft
    contract = (((1,), (1,)), ((), ()))

    wide[...] = jnp.zeros(wide.shape, F32)
    wide[0:tapst_ref.shape[0], :] = tapst_ref[...].astype(F32)
    taps_ref[...] = wide[...].T

    across_owner = jnp.broadcast_to(owner_ref[...].astype(F32), (tiles, tiles))
    down = lax.broadcasted_iota(jnp.int32, (tiles, tiles), 0)
    across_tile = lax.broadcasted_iota(jnp.int32, (tiles, tiles), 1)
    earlier = (across_owner.T == across_owner) & (down < across_tile)
    rank = jnp.sum(jnp.where(earlier, 1.0, 0.0), axis=0, keepdims=True)
    place = across_owner * TILE_DEV + rank
    order = jnp.sum(jnp.where(place == down.astype(F32), across_tile.astype(F32), 0.0), axis=1, keepdims=True)
    order = jnp.broadcast_to(order, (tiles, columns))
    loads[0].wait()
    for b in range(nblk):
        blocks[(b + 1) * dets:(b + 2) * dets, :] = x_ref[:, b * width:(b + 1) * width].astype(F32)
    blocks[(nblk + 2) * dets:, :] = jnp.zeros((blocks.shape[0] - (nblk + 2) * dets, width), F32)
    finish = exchange()
    loads[1].wait()
    for g in range(groups):
        prec[:, g * dets:(g + 1) * dets] = prec_ref[g * fd:(g + 1) * fd, :]
    finish()
    blocks[0:dets, :] = low_ref[...].astype(F32)
    blocks[(nblk + 1) * dets:(nblk + 2) * dets, :] = high_ref[...].astype(F32)
    per_row = rows_ref.shape[2] // (columns // rows_ref.shape[0])
    span = rows_ref.shape[2] // per_row
    for q in range(per_row):
        rows = jnp.concatenate([rows_ref[s][:, q * span:(q + 1) * span] for s in range(rows_ref.shape[0])], axis=1).astype(F32)
        for r in range(rows.shape[0]):
            g = r * per_row + q
            picks[g * tiles:(g + 1) * tiles, :] = jnp.where(order == rows[r:r + 1, :], 1.0, 0.0).astype(BF16)

    unroll = divisor(dets, 16)

    def filter_step(step, carry):
        for k in range(unroll):
            d = step * unroll + k
            spread = jnp.broadcast_to(taps_ref[pl.ds(d, 1), :], (width, 2 * width))
            matrix = pltpu.roll(spread, 0, 1, stride=1, stride_axis=0).astype(BF16)
            lower = blocks[pl.ds(d, padded, stride=dets), :]
            upper = blocks[pl.ds(d + dets, padded, stride=dets), :]
            window = jnp.concatenate([lower, upper], axis=1).astype(BF16)
            result[pl.ds(d, padded, stride=dets), :] = lax.dot_general(
                window, matrix, contract, preferred_element_type=F32)
        return carry

    lax.fori_loop(0, dets // unroll, filter_step, 0)

    turns = divisor(nblk + 1, 16)

    def turn_step(step, carry):
        for k in range(turns):
            b = step * turns + k
            at = pl.multiple_of(b * dets, dets)
            to = pl.multiple_of(b * width, width)
            turned[pl.ds(to, width), :] = result[pl.ds(at, dets), :].astype(BF16).T.astype(F32)
        return carry

    lax.fori_loop(0, (nblk + 1) // turns, turn_step, 0)

    share = 4

    pairs = divisor(ft // 2, 4)

    def sum_pair(pair):
        f = pair * 2
        left = turned[pl.ds(half + f, columns, stride=ft), :]
        right = turned[pl.ds(half + f + 1, columns, stride=ft), :]
        weight = jnp.concatenate([left, right], axis=1).astype(BF16)
        at = pl.multiple_of(f * tiles, tiles)
        for g in range(0, groups, share):
            sums = jnp.dot(picks[g * tiles:(g + share) * tiles, :], weight, preferred_element_type=F32).astype(BF16)
            for k in range(share):
                for side in range(2):
                    cells[pl.ds(at + side * tiles, tiles), (g + k) * dets:(g + k + 1) * dets] = (
                        sums[k * tiles:(k + 1) * tiles, side * dets:(side + 1) * dets])

    def sum_step(step, carry):
        for k in range(pairs):
            sum_pair(step * pairs + k)
        return carry

    lax.fori_loop(0, ft // 2 // pairs, sum_step, 0)

    across = LANES // fd
    low = ft // across

    def product_step(u, carry):
        parts = []
        for v in range(across):
            at = pl.multiple_of((v * low + u) * tiles, tiles)
            parts.append(lax.dot_general(cells[pl.ds(at, tiles), :], prec[...], contract, preferred_element_type=F32))
        packed[pl.ds(pl.multiple_of(u * tiles, tiles), tiles), :] = jnp.concatenate(parts, axis=1)
        return carry

    lax.fori_loop(0, low, product_step, 0, unroll=2)
    for owner in range(out_ref.shape[0]):
        mine = [packed[pl.ds(owner * TILE_DEV + k, low, stride=tiles), :] for k in range(TILE_DEV)]
        out_ref[owner] = jnp.concatenate(mine, axis=0).astype(out_ref.dtype)


def partial_scratch(half, fd, ft, tiles, x, precision):
    dets, samples = x.shape
    width = 2 * half
    padded = -(-(samples // width + 1) // 8) * 8
    groups = precision.shape[0] // fd
    across = LANES // fd
    return [
        VMEM(x.shape, BF16),
        VMEM((precision.shape[0], dets), BF16),
        pltpu.SemaphoreType.DMA((2,)),
        VMEM((2 * width, dets), F32),
        VMEM((dets, 2 * width), F32),
        VMEM(((padded + 1) * dets, width), F32),
        VMEM((padded * dets, width), F32),
        VMEM((samples + width, dets), F32),
        VMEM((groups * tiles, samples // ft), BF16),
        VMEM((fd, groups * dets), BF16),
        VMEM((ft * tiles, groups * dets), BF16),
        VMEM((ft // across * tiles, LANES), F32),
    ]


def part_shape(fd, ft, tiles):
    return (tiles // TILE_DEV, TILE_DEV * ft // (LANES // fd), LANES)


def plain_partial_sums(x, low, high, taps, rows, owner, precision, half, fd, ft, tiles):
    dets, samples = x.shape
    width = 2 * half
    groups = precision.shape[0] // fd
    blocks = samples // width
    padded = jnp.concatenate([low[:, -half:], x, high[:, :half]], axis=1).reshape(dets, blocks + 1, width)
    length = 4 * half + 1
    tiled = jnp.broadcast_to(jnp.pad(taps, ((0, 0), (0, length - taps.shape[1])))[:, None, :], (dets, width, length))
    matrix = tiled.reshape(dets, width * length)[:, :width * 2 * width].reshape(dets, width, 2 * width)
    near = jnp.einsum("dbj,dij->dbi", padded, matrix[:, :, :width], preferred_element_type=F32)
    far = jnp.einsum("dbj,dij->dbi", padded, matrix[:, :, width:], preferred_element_type=F32)
    filtered = (near[:, :-1] + far[:, 1:]).astype(BF16).reshape(dets, samples // ft, ft)
    order = jnp.argsort(owner_rows(owner)).astype(jnp.int32)
    rows = rows.reshape(rows.shape[0], groups, -1).transpose(1, 0, 2).reshape(groups, 1, -1)
    picks = (rows == order[None, :, None]).astype(BF16)
    sums = jnp.einsum("gkt,dtf->gkfd", picks, filtered, preferred_element_type=F32).astype(BF16)
    out = jnp.einsum("gkfd,gad->kfa", sums, precision.reshape(groups, fd, dets), preferred_element_type=F32)
    across = LANES // fd
    low_part = ft // across
    out = out.reshape(tiles, across, low_part, fd).transpose(0, 2, 1, 3)
    return out.reshape(tiles // TILE_DEV, TILE_DEV * low_part, LANES).astype(BF16)


def peer(me, step, n_tm, n_det):
    other = lax.rem(me + step, n_tm * n_det)
    return other, (other // n_det, lax.rem(other, n_det))


def greet(n_tm, n_det):
    me = lax.axis_index("tm") * n_det + lax.axis_index("det")
    barrier = pltpu.get_barrier_semaphore()
    for step in range(1, n_tm * n_det):
        pl.semaphore_signal(barrier, inc=1, device_id=peer(me, step, n_tm, n_det)[1], device_id_type=MESH)
    return me, barrier


def gather_body(n_tm, n_det, me, part_ref, left_ref, right_ref, out_ref, held, send_sem, recv_sem, own_sem):
    count = n_tm * n_det
    fd = left_ref.shape[0]
    copies = []
    far = range(n_det, count)
    for step in [*far, *range(1, n_det)]:
        other, where = peer(me, step, n_tm, n_det)
        copy = pltpu.make_async_remote_copy(
            src_ref=part_ref.at[other], dst_ref=held.at[me], send_sem=send_sem.at[step], recv_sem=recv_sem.at[step],
            device_id=where, device_id_type=MESH)
        copy.start()
        copies.append(copy)
    own = pltpu.make_async_copy(part_ref.at[me], held.at[me], own_sem)
    own.start()
    own.wait()
    for copy in copies:
        copy.wait()
    total = jnp.sum(held[...].astype(F32), axis=0)
    low = total.shape[0] // TILE_DEV
    across = total.shape[1] // fd
    tiles = []
    for k in range(TILE_DEV):
        tile = total[k * low:(k + 1) * low, :]
        stacked = jnp.concatenate([tile[:, v * fd:(v + 1) * fd] for v in range(across)], axis=0)
        rows = jnp.dot(stacked, left_ref[...], precision=lax.Precision.HIGHEST, preferred_element_type=F32)
        tiles.append(lax.dot_general(
            rows, right_ref[...], (((0,), (0,)), ((), ())), precision=lax.Precision.HIGHEST,
            preferred_element_type=F32))
    width = right_ref.shape[1]
    for i in range(left_ref.shape[1]):
        out_ref[:, i * width:(i + 1) * width] = jnp.concatenate([tile[i:i + 1, :] for tile in tiles], axis=0)


def gather_kernel(n_tm, n_det, part_ref, left_ref, right_ref, out_ref, *scratch):
    me, barrier = greet(n_tm, n_det)
    pl.semaphore_wait(barrier, n_tm * n_det - 1)
    gather_body(n_tm, n_det, me, part_ref, left_ref, right_ref, out_ref, *scratch)


def whole_kernel(n_tm, n_det, sizes, x_ref, taps_ref, owner_ref, prec_ref, tile_ref, left_ref, right_ref, count_ref, out_ref, part, low, high, held_rows, own_rows, *rest):
    edge, gather, scratch = rest[:5], rest[5:9], rest[9:]
    live_rows(tile_ref, count_ref, own_rows)
    me, barrier = greet(n_tm, n_det)

    def exchange():
        pl.semaphore_wait(barrier, n_tm * n_det - 1)
        return start_edges(n_tm, n_det, 2 * sizes[0], x_ref, low, high, held_rows, own_rows, *edge)

    partial_body(*sizes, exchange, x_ref, taps_ref, owner_ref, prec_ref, low, high, held_rows, part, *scratch)
    gather_body(n_tm, n_det, me, part, left_ref, right_ref, out_ref, *gather)


def gather_scratch(count, shape):
    return [
        VMEM(shape, BF16),
        pltpu.SemaphoreType.DMA((count,)),
        pltpu.SemaphoreType.DMA((count,)),
        pltpu.SemaphoreType.DMA,
    ]


def call(kernel, specs, inputs, scratch, flat, name):
    return pl.pallas_call(
        kernel,
        out_shape=jax.ShapeDtypeStruct((TILE_DEV, flat), F32),
        in_specs=[pl.BlockSpec(memory_space=space) for space in specs],
        out_specs=pl.BlockSpec(memory_space=VMEM),
        scratch_shapes=scratch,
        compiler_params=pltpu.CompilerParams(
            collective_id=1, has_side_effects=True, vmem_limit_bytes=60 * 1024 * 1024),
        name=name,
    )(*inputs)


def local(
    n_tm, n_det,
    time_stream, filter_taps, det_precision, left_weight, right_weight, frame_tile, tile_owner, frame_count,
):
    half = filter_taps.shape[1] // 2
    fd, ft = left_weight.shape[1], right_weight.shape[1]
    dets = time_stream.shape[0]
    tiles = tile_owner.shape[0]
    count = n_tm * n_det
    tile = frame_tile.reshape(-1, LANES)
    sizes = (half, fd, ft, tiles)
    shape = part_shape(fd, ft, tiles)
    flat = left_weight.shape[0] * right_weight.shape[0]
    weights = (left_weight.T, right_weight.T)
    gather = gather_scratch(count, shape)
    if dets % LANES == 0:
        inputs = (time_stream, filter_taps.T, tile_owner.reshape(1, -1), det_precision, tile) + weights + (frame_count,)
        specs = (pl.ANY, VMEM, VMEM, pl.ANY, VMEM, VMEM, VMEM, pltpu.SMEM)
        halo = VMEM((dets, 2 * half), BF16)
        scratch = [VMEM(shape, BF16), halo, halo, VMEM((n_det,) + tile.shape, tile.dtype), VMEM(tile.shape, tile.dtype)]
        scratch += edge_sems(n_det) + gather + partial_scratch(half, fd, ft, tiles, time_stream, det_precision)
        return call(functools.partial(whole_kernel, n_tm, n_det, sizes), specs, inputs, scratch, flat, "whole")
    low, high, rows = exchange_edges(n_tm, n_det, 2 * half, time_stream, tile, frame_count)
    precision = lax.dynamic_slice_in_dim(det_precision, lax.axis_index("det") * dets, dets, axis=1)
    part = plain_partial_sums(time_stream, low, high, filter_taps, rows, tile_owner, precision, *sizes)
    return call(functools.partial(gather_kernel, n_tm, n_det), (VMEM,) * 3, (part,) + weights, gather, flat, "gather")


def solution(mesh):
    return jax.shard_map(
        functools.partial(local, mesh.shape["tm"], mesh.shape["det"]),
        mesh=mesh,
        in_specs=(
            P("det", "tm"),
            P("det", None),
            P(),
            P(),
            P(),
            P(("tm", "det"), None),
            P(),
            P(("tm", "det")),
        ),
        out_specs=P(("tm", "det"), None),
        check_vma=False,
    )
```
